32 devices in a mesh: fsdp: 8 (over z, x), tp: 4 (over y, core).
Axes of the slice: x: 2, y: 2, z: 4, core: 2. Of those that a mesh axis runs over, the one named last changes fastest.
Arguments:
- tokens: bfloat16 [4096, 2048], P(('fsdp', 'tp'))
- segments: int32 [4096], P('fsdp'), may hold values from 0 to 3, as said below
- positions: int32 [4096], P('fsdp'), may hold values from 0 to 255, as said below
- gains: bfloat16 [2, 2, 2048], replicated, may hold values from 0.5 to 1.5
- w_query: bfloat16 [2, 2048, 2048], P(None, 'fsdp', 'tp'), may hold values from -1 to 1
- w_key: bfloat16 [2, 2048, 512], P(None, 'fsdp', 'tp'), may hold values from -1 to 1
- w_value: bfloat16 [2, 2048, 512], P(None, 'fsdp', 'tp'), may hold values from -0.125 to 0.125
- w_out: bfloat16 [2, 2048, 2048], P(None, 'fsdp', 'tp'), may hold values from -0.5 to 0.5
- w_gate: bfloat16 [2, 2048, 8192], P(None, 'fsdp', 'tp'), may hold values from -0.125 to 0.125
- w_up: bfloat16 [2, 2048, 8192], P(None, 'fsdp', 'tp'), may hold values from -0.125 to 0.125
- w_down: bfloat16 [2, 2048, 8192], P(None, 'fsdp', 'tp'), may hold values from -0.0625 to 0.0625
- cotangent: bfloat16 [4096, 2048], P(('fsdp', 'tp'))
Outputs:
- output: bfloat16 [4096, 2048], P(('fsdp', 'tp'))
- tokens_grad: float32 [4096, 2048], P(('fsdp', 'tp'))
- query_grad: float32 [2, 2048, 2048], P(None, 'fsdp', 'tp')
- key_grad: float32 [2, 2048, 512], P(None, 'fsdp', 'tp')
- value_grad: float32 [2, 2048, 512], P(None, 'fsdp', 'tp')
- out_grad: float32 [2, 2048, 2048], P(None, 'fsdp', 'tp')
- gate_grad: float32 [2, 2048, 8192], P(None, 'fsdp', 'tp')
- up_grad: float32 [2, 2048, 8192], P(None, 'fsdp', 'tp')
- down_grad: float32 [2, 2048, 8192], P(None, 'fsdp', 'tp')
- gains_grad: float32 [2, 2, 2048], P(None, None, ('fsdp', 'tp'))
The draws below stay inside these ranges and needn't reach their ends.
Inputs may be any that keep to these rules, and one draw needn't show every extreme that they name: `segments`: each sequence of 512 tokens (those of one index of fsdp) holds exactly 4 documents, numbered 0 to 3 in order, one of them exactly 256 tokens long. `positions`: A token's place within its document, 0 at the document's first token.
All inputs are finite; a program needn't handle non-finite values.
Results may differ from the reference program's by a relative error of at most 0.03.
Values may be sent and summed in bfloat16 or wider, within the bound.
No kernel may reach another device: no remote copies, remote signals or barrier semaphores. Data moves between devices by JAX's collectives and lax.ppermute only.
A program may use at most 256 MiB of HBM per device.

```python
import math
import jax
import jax.numpy as jnp
from jax import lax

D = 2048
HEADS = 32
KV = 8
HD = 64
FF = 8192
LAYERS = 2
QW = 2048
KW = 512
ROWS = 512
TOKENS = 4096
N_FSDP = 8


def order_one(order_key):
    return jax.random.permutation(order_key, 4)


def doc_layout(key):
    groups = TOKENS // ROWS
    half_rows = ROWS // 2
    key_first, key_second, key_order = jax.random.split(jax.random.fold_in(key, 7), 3)
    cut_first = jax.random.randint(key_first, (groups,), 1, half_rows // 2)
    cut_second = jax.random.randint(key_second, (groups,), half_rows // 2 + 1, half_rows)
    lengths = jnp.stack([jnp.full((groups,), half_rows, jnp.int32), cut_first.astype(jnp.int32), (cut_second - cut_first).astype(jnp.int32), (half_rows - cut_second).astype(jnp.int32)], 1)
    orders = jax.vmap(order_one)(jax.random.split(key_order, groups)).astype(jnp.int32)
    lengths = jnp.take_along_axis(lengths, orders, 1)
    starts = jnp.cumsum(lengths, 1) - lengths
    row_index = jnp.arange(ROWS, dtype=jnp.int32)
    segment_ids = jnp.sum((row_index[None, :, None] >= starts[:, None, 1:]).astype(jnp.int32), 2)
    doc_start = jnp.sum(jnp.where(segment_ids[:, :, None] == jnp.arange(4, dtype=jnp.int32)[None, None, :], starts[:, None, :], 0), 2)
    places = row_index[None, :] - doc_start
    return (segment_ids.reshape(TOKENS).astype(jnp.int32), places.reshape(TOKENS).astype(jnp.int32))


def draw_segments(key, part):
    return doc_layout(key)[0]


def draw_positions(key, part):
    return doc_layout(key)[1]


def draw_tokens(key, part):
    key_base, key_rows, key_cols = jax.random.split(jax.random.fold_in(key, 11), 3)
    base = jnp.clip(jax.random.normal(key_base, (TOKENS, D), jnp.float32), -4.0, 4.0)
    row_scale = jnp.exp(jax.random.uniform(key_rows, (TOKENS, 1), jnp.float32, math.log(0.3), math.log(3.0)))
    col_scale = jnp.exp(jax.random.uniform(key_cols, (1, D), jnp.float32, math.log(0.4), math.log(2.5)))
    return (base * row_scale * col_scale).astype(jnp.bfloat16)


def draw_cotangent(key, part):
    key_base = jax.random.fold_in(key, 13)
    ramp = jnp.arange(TOKENS, dtype=jnp.float32)[:, None] / TOKENS
    base = jnp.clip(jax.random.normal(key_base, (TOKENS, D), jnp.float32), -5.0, 5.0)
    return (base * (0.6 + 1.2 * ramp)).astype(jnp.bfloat16)


def projection_base(key, salt, columns):
    sub_key = jax.random.fold_in(key, salt)
    base = jnp.clip(jax.random.normal(sub_key, (LAYERS, D, columns), jnp.float32), -4.0, 4.0)
    return base * D ** (-0.5)


def draw_w_query(key, part):
    return jnp.clip(projection_base(key, 19, HEADS * HD), -1.0, 1.0).astype(jnp.bfloat16)


def draw_w_key(key, part):
    return jnp.clip(projection_base(key, 23, KV * HD), -1.0, 1.0).astype(jnp.bfloat16)


def block_scale(stream_key, shape, cuts, low, top_value):
    def one(dim, blocks):
        steps = jax.random.uniform(jax.random.fold_in(jax.random.fold_in(stream_key, 6), dim), (blocks,), jnp.float32, low / len(cuts), top_value / len(cuts))
        return jnp.repeat(jnp.exp(steps), shape[dim] // blocks).reshape((-1,) + (1,) * (len(shape) - dim - 1))

    loudness = one(*cuts[0])
    for cut in cuts[1:]:
        loudness = loudness * one(*cut)
    return loudness


def scatter_about(key, dims, spread, most, shards=(), held_as=jnp.bfloat16):
    factor_of = block_scale(key, dims, shards, -0.22, 0.18) if shards else 1.0
    values = jax.random.normal(key, dims, jnp.float32) * spread * factor_of
    return jnp.minimum(jnp.maximum(values, -most), most).astype(held_as)


def setup_inputs(seed: int = 0) -> dict:
    splits = jax.random.split(jax.random.key(seed), 13)
    return {
        "tokens": draw_tokens(jax.random.fold_in(splits[12], 71), 0),
        "segments": draw_segments(jax.random.fold_in(splits[12], 71), 0),
        "positions": draw_positions(jax.random.fold_in(splits[12], 71), 0),
        "gains": jnp.clip(1.0 + 0.1 * jax.random.normal(splits[3], (LAYERS, 2, D), jnp.float32), 0.5, 1.5).astype(jnp.bfloat16),
        "w_query": draw_w_query(jax.random.fold_in(splits[12], 71), 0),
        "w_key": draw_w_key(jax.random.fold_in(splits[12], 71), 0),
        "w_value": scatter_about(splits[6], (LAYERS, D, KW), D ** -0.5, 0.125, ((1, 8), (2, 4))),
        "w_out": scatter_about(splits[7], (LAYERS, D, QW), (QW // 16) ** -0.5, 0.5, ((1, 8), (2, 4))),
        "w_gate": scatter_about(splits[8], (LAYERS, D, FF), D ** -0.5, 0.125, ((1, 8), (2, 4))),
        "w_up": scatter_about(splits[9], (LAYERS, D, FF), D ** -0.5, 0.125, ((1, 8), (2, 4))),
        "w_down": scatter_about(splits[10], (LAYERS, D, FF), FF ** -0.5, 0.0625, ((1, 8), (2, 4))),
        "cotangent": draw_cotangent(jax.random.fold_in(splits[12], 71), 0),
    }


@jax.custom_vjp
def low(v):
    return lax.optimization_barrier(v.astype(jnp.bfloat16)).astype(jnp.float32)

@jax.custom_vjp
def low_back(v):
    return v

def low_keep(v):
    return (low(v), None)

def low_pass(kept, grad):
    return (grad,)

def back_keep(v):
    return (v, None)

def back_low(kept, grad):
    return (low(grad),)
low.defvjp(low_keep, low_pass)
low_back.defvjp(back_keep, back_low)
NORM_EPS = 1e-05
ROPE_BASE = 500000.0
MASKED = -1e+30
HIGHEST_PRECISION = lax.Precision.HIGHEST

def matmul_high(left, right):
    return jnp.dot(left, right, precision=HIGHEST_PRECISION, preferred_element_type=jnp.float32)

def matmul_back(left, right):
    return lax.dot_general(left, right, (((1,), (1,)), ((), ())), precision=HIGHEST_PRECISION, preferred_element_type=jnp.float32)

def rms_normed(hidden, gain_row):
    return hidden * lax.rsqrt(lax.optimization_barrier(jnp.mean(hidden * hidden, -1, keepdims=True)) + NORM_EPS) * gain_row

def rope_tables(positions):
    half_dim = HD // 2
    frequency = jnp.exp(-(2.0 * jnp.arange(half_dim, dtype=jnp.float32) / HD) * math.log(ROPE_BASE))
    angles = positions.astype(jnp.float32)[:, None] * frequency[None, :]
    return (jnp.cos(angles), jnp.sin(angles))

def rotate(vectors, cosines, sines):
    half_dim = vectors.shape[-1] // 2
    front_half = vectors[..., :half_dim]
    back_half = vectors[..., half_dim:]
    cos_rows = cosines[:, None, :]
    sin_rows = sines[:, None, :]
    return jnp.concatenate([front_half * cos_rows - back_half * sin_rows, back_half * cos_rows + front_half * sin_rows], -1)

def block(hidden, weights, gain_pair, seg_mask, cosines, sines):
    w_query, w_key, w_value, w_out, w_gate, w_up, w_down = weights
    group_size = HEADS // KV
    normed_first = low(rms_normed(hidden, gain_pair[0]))
    queries = low(rotate(low_back(matmul_high(normed_first, w_query)).reshape(ROWS, HEADS, HD), cosines, sines))
    queries = queries.reshape(ROWS, KV, group_size, HD)
    keys_rot = low(rotate(low_back(matmul_high(normed_first, w_key)).reshape(ROWS, KV, HD), cosines, sines))
    values = low(low_back(matmul_high(normed_first, w_value))).reshape(ROWS, KV, HD)
    scores = jnp.einsum('qkgd,skd->kgqs', queries, keys_rot, precision=HIGHEST_PRECISION) * HD ** (-0.5)
    scores = jnp.where(seg_mask, low_back(scores), MASKED)
    probs = jax.nn.softmax(scores, axis=-1)
    attended = jnp.einsum('kgqs,skd->qkgd', low(probs), values, precision=HIGHEST_PRECISION).reshape(ROWS, HEADS * HD)
    attended = low(low_back(attended))
    mid_rows = hidden + low_back(matmul_back(attended, w_out))
    normed_second = low(rms_normed(mid_rows, gain_pair[1]))
    gate_act = low_back(matmul_high(normed_second, w_gate))
    up_act = low_back(matmul_high(normed_second, w_up))
    mixed_rows = low(jax.nn.silu(gate_act) * up_act)
    return mid_rows + low_back(matmul_back(mixed_rows, w_down))

def reference(tokens, segments, positions, gains, w_query, w_key, w_value, w_out, w_gate, w_up, w_down, cotangent):
    weights = tuple((weight.astype(jnp.float32) for weight in (w_query, w_key, w_value, w_out, w_gate, w_up, w_down)))
    gain_rows = gains.astype(jnp.float32)
    inputs = tokens.astype(jnp.float32).reshape(N_FSDP, ROWS, D)
    seg_rows = segments.reshape(N_FSDP, ROWS)
    pos_rows = positions.reshape(N_FSDP, ROWS)
    row_index = jnp.arange(ROWS, dtype=jnp.int32)

    def forward(weights, gain_rows, inputs):

        def one_sequence(packed):
            hidden, seg_row, pos_row = packed
            cosines, sines = rope_tables(pos_row)
            seg_mask = (seg_row[:, None] == seg_row[None, :]) & (row_index[None, :] <= row_index[:, None])
            for layer_index in range(LAYERS):
                hidden = block(hidden, tuple((weight[layer_index] for weight in weights)), gain_rows[layer_index], seg_mask, cosines, sines)
            return hidden
        return lax.map(jax.checkpoint(one_sequence), (inputs, seg_rows, pos_rows))
    outputs, pullback = jax.vjp(forward, weights, gain_rows, inputs)
    weight_grads, gain_grads, input_grads = pullback(cotangent.astype(jnp.float32).reshape(N_FSDP, ROWS, D))
    return (outputs.reshape(TOKENS, D).astype(jnp.bfloat16), input_grads.reshape(TOKENS, D), weight_grads[0], weight_grads[1], weight_grads[2], weight_grads[3], weight_grads[4], weight_grads[5], weight_grads[6], gain_grads)
```

```python
import math

import jax
import jax.numpy as jnp
from jax import lax
from jax.sharding import PartitionSpec as P

HEADS = 32
KV = 8
HD = 64

NORM_EPS = 1e-05
ROPE_BASE = 500000.0
MASKED = -1e30

BIT_C = 1
BIT_B = 2
BIT_A = 4
BIT_CORE = 1
BIT_Y = 2


def swap_fsdp(value, bit):
    count = lax.axis_size("fsdp")
    return lax.ppermute(value, "fsdp", [(i, i ^ bit) for i in range(count)])


def swap_tp(value, bit):
    count = lax.axis_size("tp")
    return lax.ppermute(value, "tp", [(i, i ^ bit) for i in range(count)])


def flip_if(value, axis, flag):
    low = lax.slice_in_dim(value, 0, 1, axis=axis)
    high = lax.slice_in_dim(value, 1, 2, axis=axis)
    return jnp.where(
        flag, jnp.concatenate([high, low], axis), jnp.concatenate([low, high], axis)
    )


class Place:
    def __init__(self, width):
        self.f = lax.axis_index("fsdp")
        self.t = lax.axis_index("tp")
        self.c = self.f % 2
        self.b = (self.f // 2) % 2
        self.a_bits = (lax.axis_size("fsdp") // 4).bit_length() - 1
        self.rows = width // lax.axis_size("fsdp")

    def _flip_a(self, value, axis):
        shape = value.shape
        bits = self.a_bits
        if bits == 0:
            return value
        value = value.reshape(shape[:axis] + (2,) * bits + shape[axis + 1 :])
        for k in range(bits):
            value = flip_if(value, axis + bits - 1 - k, ((self.f // (BIT_A << k)) % 2) == 1)
        return value.reshape(shape)

    def to_local(self, value):
        lead = value.shape[:-1]
        n = len(lead)
        value = value.reshape(lead + (1 << self.a_bits, 2, 2, self.rows))
        value = flip_if(value, n + 2, self.c == 1)
        value = self._flip_a(value, n)
        order = tuple(range(n)) + (n + 2, n, n + 1, n + 3)
        return value.transpose(order).reshape(lead + (-1,))

    def to_global(self, value):
        lead = value.shape[:-1]
        n = len(lead)
        value = value.reshape(lead + (2, 1 << self.a_bits, 2, self.rows))
        order = tuple(range(n)) + (n + 1, n + 2, n, n + 3)
        value = value.transpose(order)
        value = flip_if(value, n + 2, self.c == 1)
        value = self._flip_a(value, n)
        return value.reshape(lead + (-1,))

    def quarters(self, value):
        value = value.reshape(2, 2, -1)
        value = flip_if(value, 0, (self.t // 2) == 1)
        value = flip_if(value, 1, (self.t % 2) == 1)
        return value.transpose(1, 0, 2).reshape(-1)

    def halves(self, weight):
        half = weight.shape[-1] // 2
        keep = lax.dynamic_slice_in_dim(weight, self.b * half, half, axis=weight.ndim - 1)
        give = lax.dynamic_slice_in_dim(weight, (1 - self.b) * half, half, axis=weight.ndim - 1)
        return keep, give

    def gather_weight(self, keep, give):
        other = swap_fsdp(give, BIT_B)
        pair = jnp.where(
            self.b == 0, jnp.concatenate([keep, other], 0), jnp.concatenate([other, keep], 0)
        )
        blocks = [pair]
        for k in range(self.a_bits):
            blocks = blocks + [swap_fsdp(block, BIT_A << k) for block in blocks]
        blocks = blocks + [swap_fsdp(block, BIT_C) for block in blocks]
        return jnp.concatenate(blocks, 0)

    def reduce_weight(self, left, right):
        width = left.shape[1]

        def part(start, count, others):
            total = contract_rows(left[:, start : start + count], right)
            for other in others:
                total = total + other[start : start + count].astype(jnp.float32)
            return total

        count = width // 2
        others = [swap_fsdp(part(count, count, []).astype(jnp.bfloat16), BIT_C)]
        for k in reversed(range(self.a_bits)):
            count //= 2
            sent = part(count, count, others).astype(jnp.bfloat16)
            others.append(swap_fsdp(sent, BIT_A << k))
        own = part(0, count, others).reshape(2, self.rows, -1)
        keep = lax.dynamic_index_in_dim(own, self.b, 0, keepdims=False)
        give = lax.dynamic_index_in_dim(own, 1 - self.b, 0, keepdims=False)
        got = swap_fsdp(give.astype(jnp.bfloat16), BIT_B).astype(jnp.float32)
        return keep, got

    def join(self, keep, got):
        return jnp.where(
            self.b == 0, jnp.concatenate([keep, got], 1), jnp.concatenate([got, keep], 1)
        )


def rope_tables(positions, head_dim):
    half_dim = head_dim // 2
    frequency = jnp.exp(
        -(2.0 * jnp.arange(half_dim, dtype=jnp.float32) / head_dim) * math.log(ROPE_BASE)
    )
    angles = positions.astype(jnp.float32)[:, None] * frequency[None, :]
    return (jnp.cos(angles), jnp.sin(angles))


def rotate(vectors, cosines, sines):
    half_dim = vectors.shape[-1] // 2
    front_half = vectors[..., :half_dim]
    back_half = vectors[..., half_dim:]
    cos_rows = cosines[:, None, :]
    sin_rows = sines[:, None, :]
    return jnp.concatenate(
        [
            front_half * cos_rows - back_half * sin_rows,
            back_half * cos_rows + front_half * sin_rows,
        ],
        -1,
    )


def gather_rows(rows):
    half = rows.shape[0] // 2
    by_y = swap_tp(rows, BIT_Y)
    by_b = swap_fsdp(rows, BIT_B)
    both = [swap_tp(by_b[:half], BIT_Y), swap_fsdp(by_y[half:], BIT_B)]
    blocks = [rows, by_y, by_b] + both
    return jnp.concatenate(blocks + [swap_tp(block, BIT_CORE) for block in blocks], 0)


def reduce_rows(term_fn, count):
    low = jnp.bfloat16
    got = swap_tp(term_fn(4 * count, 4 * count).astype(low), BIT_CORE)
    mine = term_fn(0, 4 * count) + got.astype(jnp.float32)
    half = count // 2
    far = mine[3 * count :].astype(low)
    far_y = swap_tp(far[:half], BIT_Y).astype(jnp.float32)
    far_b = swap_fsdp(far[half:], BIT_B).astype(jnp.float32)
    to_y = mine[count : 2 * count]
    to_b = mine[2 * count : 3 * count]
    to_y = jnp.concatenate([to_y[:half], to_y[half:] + far_b], 0).astype(low)
    to_b = jnp.concatenate([to_b[:half] + far_y, to_b[half:]], 0).astype(low)
    from_y = swap_tp(to_y, BIT_Y).astype(jnp.float32)
    from_b = swap_fsdp(to_b, BIT_B).astype(jnp.float32)
    return mine[:count] + from_y + from_b


def project_rows(pairs):
    def term(start, count):
        total = None
        for left, right in pairs:
            row_term = lax.dot_general(
                left[start : start + count],
                right,
                (((1,), (1,)), ((), ())),
                preferred_element_type=jnp.float32,
            )
            total = row_term if total is None else total + row_term
        return total

    return term


def contract_rows(left_rows, right_rows):
    return lax.dot_general(
        left_rows, right_rows, (((0,), (0,)), ((), ())), preferred_element_type=jnp.float32
    )


def multiply(left, right):
    return jnp.dot(left, right, preferred_element_type=jnp.float32)


def inverse_rms(hidden):
    return lax.rsqrt(jnp.mean(hidden * hidden, -1, keepdims=True) + NORM_EPS)


def norm_back(hidden, inv_rms, gain_row, grad_out):
    unit_rows = hidden * inv_rms
    gain_part = jnp.sum(grad_out * unit_rows, 0)
    grad_unit = grad_out * gain_row
    grad_in = inv_rms * (grad_unit - unit_rows * jnp.mean(grad_unit * unit_rows, -1, keepdims=True))
    return (grad_in, gain_part)


def score_rows(queries, keys_rot, seg_mask, score_scale):
    scores = (
        jnp.einsum("zqgd,zsd->zgqs", queries, keys_rot, preferred_element_type=jnp.float32)
        * score_scale
    )
    return jnp.where(seg_mask, scores, MASKED)


def attend(queries, keys_rot, values, seg_mask, score_scale):
    scores = score_rows(queries, keys_rot, seg_mask, score_scale)
    row_max = jnp.max(scores, -1, keepdims=True)
    exp_scores = jnp.exp(scores - row_max)
    row_total = jnp.sum(exp_scores, -1, keepdims=True)
    probs = (exp_scores / row_total).astype(jnp.bfloat16)
    attended = jnp.einsum("zgqs,zsd->zqgd", probs, values, preferred_element_type=jnp.float32)
    return (attended, row_max + jnp.log(row_total))


def attend_back(queries, keys_rot, values, log_total, grad_out, seg_mask, score_scale):
    probs = jnp.exp(score_rows(queries, keys_rot, seg_mask, score_scale) - log_total)
    grad_values = jnp.einsum(
        "zgqs,zqgd->zsd", probs.astype(jnp.bfloat16), grad_out, preferred_element_type=jnp.float32
    )
    grad_probs = jnp.einsum("zqgd,zsd->zgqs", grad_out, values, preferred_element_type=jnp.float32)
    grad_scores = (probs * (grad_probs - jnp.sum(grad_probs * probs, -1, keepdims=True))).astype(
        jnp.bfloat16
    )
    grad_queries = (
        jnp.einsum("zgqs,zsd->zqgd", grad_scores, keys_rot, preferred_element_type=jnp.float32)
        * score_scale
    )
    grad_keys = (
        jnp.einsum("zgqs,zqgd->zsd", grad_scores, queries, preferred_element_type=jnp.float32)
        * score_scale
    )
    return (grad_queries, grad_keys, grad_values)


def by_sequence(rows):
    width = rows.shape[-1]
    return rows.reshape(2, 2, -1, width).transpose(1, 0, 2, 3).reshape(2, -1, width)


def by_block(rows):
    width = rows.shape[-1]
    return rows.reshape(2, 2, -1, width).transpose(1, 0, 2, 3).reshape(-1, width)


def scatter_sum(value):
    f = lax.axis_index("fsdp")
    t = lax.axis_index("tp")
    for swap, index, size in ((swap_fsdp, f, lax.axis_size("fsdp")), (swap_tp, t, lax.axis_size("tp"))):
        bit = size // 2
        while bit:
            half = value.shape[-1] // 2
            mine = (index // bit) % 2
            keep = lax.dynamic_slice_in_dim(value, mine * half, half, axis=value.ndim - 1)
            give = lax.dynamic_slice_in_dim(value, (1 - mine) * half, half, axis=value.ndim - 1)
            value = keep + swap(give, bit)
            bit //= 2
    return value


def on_device(
    tokens,
    segments,
    positions,
    gains,
    w_query,
    w_key,
    w_value,
    w_out,
    w_gate,
    w_up,
    w_down,
    cotangent,
):
    tok_rows = tokens.shape[0]
    layers = w_query.shape[0]
    place = Place(tokens.shape[1])
    score_scale = HD ** (-0.5)
    qw = w_query.shape[2] // 2
    kw = w_key.shape[2] // 2
    groups = qw // HD
    low = jnp.bfloat16

    weights = []
    for layer in range(layers):
        parts = [place.halves(w[layer]) for w in (w_query, w_key, w_value)]
        qkv = place.gather_weight(
            jnp.concatenate([p[0] for p in parts], 1), jnp.concatenate([p[1] for p in parts], 1)
        )
        rest = [place.gather_weight(*place.halves(w[layer])) for w in (w_out, w_gate, w_up, w_down)]
        weights.append((qkv, *rest))

    seq = jnp.stack([segments, positions])
    seq = jnp.stack([seq, swap_fsdp(seq, BIT_B)])
    seg_rows = jnp.stack([place.quarters(seq[i, 0]) for i in range(2)])
    pos_rows = jnp.stack([place.quarters(seq[i, 1]) for i in range(2)])
    order = place.quarters(jnp.arange(segments.shape[0]))
    seg_mask = (
        (seg_rows[:, :, None] == seg_rows[:, None, :]) & (order[None, None, :] <= order[None, :, None])
    )[:, None]
    cosines, sines = rope_tables(pos_rows.reshape(-1), HD)
    gain_rows = place.to_local(gains.astype(jnp.float32))
    hidden = place.to_local(tokens).astype(jnp.float32)
    grad_rows = place.to_local(cotangent).astype(jnp.float32)

    saved_layers = []
    for layer in range(layers):
        qkv_full, wo_full, wg_full, wu_full, wd_full = weights[layer]
        inv_first = inverse_rms(hidden)
        normed_first = gather_rows((hidden * inv_first * gain_rows[layer, 0]).astype(low))
        lin = by_sequence(multiply(normed_first, qkv_full))
        lin = lin.reshape(-1, lin.shape[-1])
        queries = rotate(lin[:, :qw].reshape(-1, groups, HD), cosines, sines)
        queries = queries.astype(low).reshape(2, -1, groups, HD)
        keys_rot = rotate(lin[:, qw : qw + kw].reshape(-1, 1, HD), cosines, sines)
        keys_rot = keys_rot.astype(low).reshape(2, -1, HD)
        values = lin[:, qw + kw :].astype(low).reshape(2, -1, HD)
        attended, log_total = attend(queries, keys_rot, values, seg_mask, score_scale)
        attended = by_block(attended.astype(low).reshape(2, -1, qw))
        mid_rows = hidden + reduce_rows(project_rows([(attended, wo_full)]), tok_rows)
        inv_second = inverse_rms(mid_rows)
        normed_second = gather_rows((mid_rows * inv_second * gain_rows[layer, 1]).astype(low))
        gate_act = multiply(normed_second, wg_full)
        up_act = multiply(normed_second, wu_full)
        mixed_rows = (jax.nn.silu(gate_act) * up_act).astype(low)
        after_rows = mid_rows + reduce_rows(project_rows([(mixed_rows, wd_full)]), tok_rows)
        saved_layers.append(
            (
                hidden,
                inv_first,
                normed_first,
                queries,
                keys_rot,
                values,
                log_total,
                attended,
                mid_rows,
                inv_second,
                normed_second,
                gate_act,
                up_act,
                mixed_rows,
            )
        )
        hidden = after_rows
    output = place.to_global(hidden.astype(low))

    weight_parts = [None] * layers
    gain_parts = [None] * layers
    for layer in reversed(range(layers)):
        qkv_full, wo_full, wg_full, wu_full, wd_full = weights[layer]
        (
            hidden,
            inv_first,
            normed_first,
            queries,
            keys_rot,
            values,
            log_total,
            attended,
            mid_rows,
            inv_second,
            normed_second,
            gate_act,
            up_act,
            mixed_rows,
        ) = saved_layers[layer]
        grad_mixed = gather_rows(grad_rows.astype(low))
        grad_z = multiply(grad_mixed, wd_full)
        sigmoid_gate = jax.nn.sigmoid(gate_act)
        grad_gate = (
            grad_z * up_act * sigmoid_gate * (1.0 + gate_act * (1.0 - sigmoid_gate))
        ).astype(low)
        grad_up = (grad_z * gate_act * sigmoid_gate).astype(low)
        down_out = place.reduce_weight(grad_mixed, mixed_rows)
        gate_out = place.reduce_weight(normed_second, grad_gate)
        up_out = place.reduce_weight(normed_second, grad_up)
        grad_second = reduce_rows(
            project_rows([(grad_gate, wg_full), (grad_up, wu_full)]), tok_rows
        )
        grad_norm_mid, gain_second = norm_back(
            mid_rows, inv_second, gain_rows[layer, 1], grad_second
        )
        grad_mid = grad_rows + grad_norm_mid
        grad_attn = gather_rows(grad_mid.astype(low))
        grad_attended = multiply(grad_attn, wo_full).astype(low)
        out_out = place.reduce_weight(grad_attn, attended)
        grad_queries, grad_keys, grad_values = attend_back(
            queries,
            keys_rot,
            values,
            log_total,
            by_sequence(grad_attended).reshape(2, -1, groups, HD),
            seg_mask,
            score_scale,
        )
        grad_lin = jnp.concatenate(
            [
                rotate(grad_queries.reshape(-1, groups, HD), cosines, -sines)
                .reshape(2, -1, qw)
                .astype(low),
                rotate(grad_keys.reshape(-1, 1, HD), cosines, -sines)
                .reshape(2, -1, kw)
                .astype(low),
                grad_values.reshape(2, -1, kw).astype(low),
            ],
            -1,
        )
        grad_lin = by_block(grad_lin)
        qkv_out = place.reduce_weight(normed_first, grad_lin)
        grad_first = reduce_rows(project_rows([(grad_lin, qkv_full)]), tok_rows)
        grad_norm_in, gain_first = norm_back(
            hidden, inv_first, gain_rows[layer, 0], grad_first
        )
        grad_rows = grad_mid + grad_norm_in
        gain_parts[layer] = jnp.stack([gain_first, gain_second])
        cuts = ((0, qw), (qw, qw + kw), (qw + kw, qw + 2 * kw))
        weight_parts[layer] = [
            place.join(qkv_out[0][:, lo:hi], qkv_out[1][:, lo:hi]) for lo, hi in cuts
        ] + [place.join(*pair) for pair in (out_out, gate_out, up_out, down_out)]
    stacked = [
        jnp.stack([weight_parts[layer][slot] for layer in range(layers)]) for slot in range(7)
    ]
    gain_total = scatter_sum(place.to_global(jnp.stack(gain_parts)))
    return (output, place.to_global(grad_rows), *stacked, gain_total)


def solution(mesh):
    rows = P(("fsdp", "tp"), None)
    weight = P(None, "fsdp", "tp")
    return jax.shard_map(
        on_device,
        mesh=mesh,
        in_specs=(rows, P("fsdp"), P("fsdp"), P()) + (weight,) * 7 + (rows,),
        out_specs=(rows, rows) + (weight,) * 7 + (P(None, None, ("fsdp", "tp")),),
        check_vma=False,
    )
```
